32 devices in a mesh: dp: 2 (over core), expert: 4 (over y, x), tensor: 4 (over z).
Axes of the slice: x: 2, y: 2, z: 4, core: 2. Of those that a mesh axis runs over, the one named last changes fastest.
Arguments:
- tokens: bfloat16 [256, 5120], P(('dp', 'expert'), 'tensor'), may hold values from -50 to 50
- expert_ids: int32 [256, 2], P(('dp', 'expert')), may hold values from 0 to 3, all different within a row; in each aligned block of 32 rows (0 to 31, 32 to 63, ...) at most 32 rows name the same one
- gate_weights: float32 [256, 2], P(('dp', 'expert')), may hold values from 0.1 to 1
- t_gate: bfloat16 [4, 5120, 8192], P('expert', None, ('dp', 'tensor')), may hold values from -0.078125 to 0.078125
- t_up: bfloat16 [4, 5120, 8192], P('expert', None, ('dp', 'tensor')), may hold values from -0.078125 to 0.078125
- t_down: bfloat16 [4, 8192, 5120], P('expert', ('dp', 'tensor')), may hold values from -0.09375 to 0.09375
- s_gate: bfloat16 [5120, 8192], P(None, ('expert', 'tensor')), may hold values from -0.078125 to 0.078125
- s_up: bfloat16 [5120, 8192], P(None, ('expert', 'tensor')), may hold values from -0.078125 to 0.078125
- s_down: bfloat16 [8192, 5120], P(('expert', 'tensor')), may hold values from -0.09375 to 0.09375
Outputs:
- grad_gate: bfloat16 [5120, 8192], P(None, ('expert', 'tensor'))
- grad_up: bfloat16 [5120, 8192], P(None, ('expert', 'tensor'))
- grad_down: bfloat16 [8192, 5120], P(('expert', 'tensor'))
- loss: float32 [], replicated
The draws below stay inside these ranges and needn't reach their ends.
Inputs may be any that keep to these rules, and one draw needn't show every extreme that they name: `expert_ids`: in each aligned block of 32 tokens no expert is named by more than 32 tokens; a token's two experts differ.
All inputs are finite; a program needn't handle non-finite values.
Results may differ from the reference program's by a relative error of at most 0.018.
Values may be sent and summed in bfloat16 or wider, within the bound.
No kernel may reach another device: no remote copies, remote signals or barrier semaphores. Data moves between devices by JAX's collectives and lax.ppermute only.
A program may use at most 128 MiB of HBM per device.

```python
import math
import jax
import jax.numpy as jnp
import numpy as np
from jax import lax

D = 5120
FFT = 8192
FFS = 8192
TOK_GRP = 32
EXPERTS = 4
CAP = 32
TOKENS = 256
N_DP = 2
N_TENSOR = 4


def draw_tokens(key, part):
    pieces = jax.random.split(jax.random.fold_in(key, 11), 3)
    positions = jnp.arange(TOKENS, dtype=jnp.float32)
    rising = jnp.exp(0.25 * jnp.log(3.0) * positions / max(TOKENS - 1, 1))
    columns = jnp.exp(jax.random.uniform(pieces[2], (1, D), jnp.float32, jnp.log(0.6), jnp.log(1.6)))
    base = jnp.clip(jax.random.normal(pieces[0], (TOKENS, D), jnp.float32), -6.0, 6.0)
    values = base * rising[:, None] * columns
    return values.astype(jnp.bfloat16)


def with_spikes(array, key, source, target, parts, factor):
    def block_of(dim):
        return (jnp.arange(array.shape[dim]) // (array.shape[dim] // parts)).reshape((-1,) + (1,) * (array.ndim - 1 - dim))

    near = jax.random.permutation(key, parts)[block_of(target)]
    far = (block_of(target) + parts // 2) % parts
    return jnp.where((block_of(source) == near) | (block_of(source) == far), factor * array, array)


def shard_levels(rng, extent, cuts, least, top_value):
    loudness, own = 1.0, jax.random.fold_in(rng, 6)
    for position, parts in cuts:
        steps = jnp.exp(jax.random.uniform(jax.random.fold_in(own, position), (parts,), jnp.float32, least / len(cuts), top_value / len(cuts)))
        loudness = loudness * jnp.repeat(steps, extent[position] // parts).reshape([-1 if axis == position else 1 for axis in range(len(extent))])
    return loudness


def routed_block(stream_key, own, number, rows, number_of, top, limit, skew):
    ranking = jax.random.permutation(stream_key, number_of)
    packed, usual = shares(number_of, rows * top, limit, skew, True), shares(number_of, rows * top, limit, skew, False)
    places = jnp.arange(number_of)

    def named(lengths, rotation):
        used = int((lengths > 0).sum())
        fixed = max(1, used // 4)
        shifted = fixed + (places - fixed + rotation * (used - fixed)) % max(1, number_of - fixed)
        return jnp.zeros((number_of,), jnp.int32).at[ranking[jnp.where(places < fixed, places, shifted)]].set(jnp.asarray(lengths, jnp.int32))

    lengths = jnp.where(number % 4 == 0, named(packed, number // 4), named(usual, number - number // 4 - 1))
    mixed = jax.random.permutation(jax.random.fold_in(own, 3), number_of)
    donor, sink = mixed[0:number_of // 2 * 2:2], mixed[1:number_of // 2 * 2:2]
    room = jnp.minimum(lengths[donor] - 1, limit - lengths[sink]) // 2
    room = jnp.where((donor == ranking[0]) | (sink == ranking[0]) | (lengths[sink] == 0), 0, jnp.maximum(room, 0))
    shifted = jax.random.randint(jax.random.fold_in(own, 4), (number_of // 2,), 0, 1 << 20) % (room + 1)
    lengths = lengths.at[donor].add(-shifted).at[sink].add(shifted)
    items = jnp.searchsorted(jnp.cumsum(lengths), jnp.arange(rows * top), side="right").astype(jnp.int32)
    grid = items.reshape(top, rows).T
    grid = grid[jax.random.permutation(jax.random.fold_in(own, 1), rows)]
    rotation = jax.random.randint(jax.random.fold_in(own, 2), (rows, 1), 0, top)
    return jnp.take_along_axis(grid, (jnp.arange(top)[None, :] + rotation) % top, axis=1)


def shares(count, total, most, lean, full):
    weights = [(1 << 20) // math.isqrt(rank ** lean) + 1 for rank in range(1, count + 1)]
    largest = most if full else min(most, max(-(-total // count), total * weights[0] // sum(weights)))
    least = 1 if total - largest >= count - 1 else 0
    given, spare = [largest] + [least] * (count - 1), total - largest - least * (count - 1)
    while spare > 0:
        movable = [i for i in range(1, count) if given[i] < largest] or [i for i in range(1, count) if given[i] < most]
        whole, remaining = sum([weights[i] for i in movable]), spare
        for i in movable:
            extra = min(most - given[i], max(1, remaining * weights[i] // whole), spare)
            given[i] = given[i] + extra
            spare = spare - extra
    return np.array(given)


def gaussian(key, dims, width, bound, cuts=(), kind=jnp.bfloat16):
    entries = width * jax.random.normal(key, dims, jnp.float32)
    if cuts:
        entries = entries * shard_levels(key, dims, cuts, -0.22, 0.18)
    return jnp.clip(entries, -bound, bound).astype(kind)


def gaussian_with(own_key, extent, scale, reach, cuts, heavy, kind=jnp.bfloat16):
    entries = scale * jax.random.normal(own_key, extent, jnp.float32)
    if cuts:
        entries = entries * shard_levels(own_key, extent, cuts, -0.22, 0.18)
    return jnp.clip(with_spikes(entries, jax.random.fold_in(own_key, 3), *heavy), -reach, reach).astype(kind)


def setup_inputs(seed: int = 0) -> dict:
    key_list = jax.random.split(jax.random.key(seed), 10)
    tokens = draw_tokens(jax.random.fold_in(key_list[9], 71), 0)
    expert_ids_keys = jax.random.split(jax.random.fold_in(key_list[1], 1), TOKENS // TOK_GRP)
    expert_ids_turns = jax.random.permutation(jax.random.fold_in(key_list[1], 3), TOKENS // TOK_GRP)
    expert_ids = jax.vmap(lambda own, number: routed_block(jax.random.fold_in(key_list[1], 2), own, number, TOK_GRP, EXPERTS, 2, CAP, 1))(expert_ids_keys, expert_ids_turns).reshape((TOKENS, 2))
    gate_weights = jnp.clip(jnp.exp(math.log(1.0) - 2.3025851 * jax.random.uniform(key_list[2], (TOKENS, 2), jnp.float32) ** shard_levels(key_list[2], (TOKENS, 2), ((0, 8),), -0.2, 0.2)), 0.1, 1.0)
    t_gate = gaussian(key_list[3], (EXPERTS, D, FFT), D ** -0.5, 0.078125, ((0, 4), (2, 8)))
    t_up = gaussian(key_list[4], (EXPERTS, D, FFT), D ** -0.5, 0.078125, ((0, 4), (2, 8)))
    t_down = gaussian_with(key_list[5], (EXPERTS, FFT, D), FFT ** -0.5, 0.09375, ((0, 4), (1, 8)), (1, 2, 8, 2.0))
    s_gate = gaussian(key_list[6], (D, FFS), D ** -0.5, 0.078125, ((1, 16),))
    s_up = gaussian(key_list[7], (D, FFS), D ** -0.5, 0.078125, ((1, 16),))
    s_down = gaussian_with(key_list[8], (FFS, D), FFS ** -0.5, 0.09375, ((0, 16),), (0, 1, 16, 2.0))
    return dict(tokens=tokens, expert_ids=expert_ids, gate_weights=gate_weights, t_gate=t_gate, t_up=t_up, t_down=t_down, s_gate=s_gate, s_up=s_up, s_down=s_down)


def pair_slots(route_ids):
    flat_ids = route_ids.reshape(-1)
    onehot = (flat_ids[:, None] == jnp.arange(EXPERTS, dtype=jnp.int32)[None, :]).astype(jnp.int32)
    before = jnp.cumsum(onehot, axis=0) - onehot
    slot_rank = lax.optimization_barrier(jnp.sum(before * onehot, axis=1))
    return (flat_ids * CAP + slot_rank).reshape(route_ids.shape)

def reference(tokens, expert_ids, gate_weights, t_gate, t_up, t_down, s_gate, s_up, s_down):
    groups = TOKENS // TOK_GRP
    shards = N_DP * N_TENSOR
    pair_codes = jax.vmap(pair_slots)(expert_ids.reshape(groups, TOK_GRP, 2))
    slot_codes = jnp.arange(EXPERTS * CAP, dtype=jnp.int32)
    group_tokens = tokens.reshape(groups, TOK_GRP, D)

    def dispatch(operands):
        group_x, codes = operands
        placing = lax.optimization_barrier(jnp.sum((codes[None, :, :] == slot_codes[:, None, None]).astype(jnp.float32), axis=2))
        return jnp.dot(placing.astype(jnp.bfloat16), group_x, preferred_element_type=jnp.float32).astype(jnp.bfloat16)
    sent = lax.map(dispatch, (group_tokens, pair_codes))
    expert_rows = sent.reshape(groups, EXPERTS, CAP, D).transpose(1, 0, 2, 3).reshape(EXPERTS, groups * CAP, D)

    def expert_apply(operands):
        rows_in, w_gate, w_up, w_down = operands
        gate_pre = jnp.dot(rows_in, w_gate, preferred_element_type=jnp.float32)
        up_pre = jnp.dot(rows_in, w_up, preferred_element_type=jnp.float32)
        activation = (gate_pre * jax.nn.sigmoid(gate_pre) * up_pre).astype(jnp.bfloat16)
        act_split = activation.reshape(groups * CAP, shards, FFT // shards).transpose(1, 0, 2).astype(jnp.float32)
        down_split = w_down.reshape(shards, FFT // shards, D).astype(jnp.float32)
        partial_value = jnp.einsum('srf,sfd->srd', act_split, down_split)
        rounded = lax.optimization_barrier(partial_value.astype(jnp.bfloat16))
        return lax.optimization_barrier(jnp.sum(rounded.astype(jnp.float32), axis=0)).astype(jnp.bfloat16)
    expert_out = lax.map(expert_apply, (expert_rows, t_gate, t_up, t_down))
    back = expert_out.reshape(EXPERTS, groups, CAP, D).transpose(1, 0, 2, 3).reshape(groups, EXPERTS * CAP, D)
    weighting = gate_weights / lax.optimization_barrier(jnp.sum(gate_weights, axis=1, keepdims=True))
    weighting = weighting.reshape(groups, TOK_GRP, 2)

    def combine(operands):
        codes, weights_here, outputs = operands
        mixing = lax.optimization_barrier(jnp.sum(weights_here[:, :, None] * (codes[:, :, None] == slot_codes[None, None, :]).astype(jnp.float32), axis=1))
        return jnp.dot(mixing, outputs.astype(jnp.float32), precision=lax.Precision.HIGHEST)
    teacher_out = lax.map(combine, (pair_codes, weighting, back)).reshape(TOKENS, D)
    gate_pre = jnp.dot(tokens, s_gate, preferred_element_type=jnp.float32)
    up_pre = jnp.dot(tokens, s_up, preferred_element_type=jnp.float32)
    gate_sig = jax.nn.sigmoid(gate_pre)
    activation = (gate_pre * gate_sig * up_pre).astype(jnp.bfloat16)
    student_out = jnp.dot(activation, s_down, preferred_element_type=jnp.float32)
    residual = student_out - teacher_out
    loss_value = jnp.sum(residual * residual) / (TOKENS * D)
    grad_scale = 1.0 / math.sqrt(TOKENS)
    d_out = (residual * grad_scale).astype(jnp.bfloat16)
    d_act = jnp.dot(d_out, s_down.T, preferred_element_type=jnp.float32)
    d_down = jnp.dot(activation.T, d_out, preferred_element_type=jnp.float32)
    d_gate_pre = (d_act * up_pre * gate_sig * (1.0 + gate_pre * (1.0 - gate_sig))).astype(jnp.bfloat16)
    d_up_pre = (d_act * gate_pre * gate_sig).astype(jnp.bfloat16)
    d_gate = jnp.dot(tokens.T, d_gate_pre, preferred_element_type=jnp.float32)
    d_up = jnp.dot(tokens.T, d_up_pre, preferred_element_type=jnp.float32)
    return (d_gate.astype(jnp.bfloat16), d_up.astype(jnp.bfloat16), d_down.astype(jnp.bfloat16), loss_value)
```

```python
import functools
import math

import jax
import jax.numpy as jnp
from jax import lax
from jax.experimental import pallas as pl
from jax.experimental.pallas import tpu as pltpu
from jax.sharding import PartitionSpec as P

BF = jnp.bfloat16
F32 = jnp.float32
ANY = pl.BlockSpec(memory_space=pl.ANY)
VMEM_LIMIT = 60 * 1024 * 1024


def swap(x, axis, n, r):
    return lax.ppermute(x, axis, [(i, i ^ r) for i in range(n)])


def tile_of(n, most):
    t = min(n, most)
    while n % t:
        t //= 2
    return t


def cost(flops, moved):
    return pl.CostEstimate(flops=int(flops), bytes_accessed=int(moved), transcendentals=0)


def params(n=1):
    return pltpu.CompilerParams(
        dimension_semantics=("arbitrary",) * n, vmem_limit_bytes=VMEM_LIMIT
    )


def dot(a, b):
    return jnp.dot(a, b, preferred_element_type=F32)


def up_kernel(nd, ne, nz, rows, width, steps_t, sc, w_ref, tg, tu, sg, su, *rest):
    pieces = rest[: nd * ne]
    at_ref, act_ref, f1_ref, f2_ref, xs, sem = rest[nd * ne :]
    step = pl.program_id(0)

    @pl.when(step == 0)
    def _():
        copies = []
        for a in range(nd):
            for b in range(ne):
                for j in range(nz):
                    row = pl.multiple_of((b * nd + (sc[0] ^ a)) * rows, rows)
                    col = pl.multiple_of((sc[2] ^ j) * width, 128)
                    copies.append(
                        pltpu.make_async_copy(
                            pieces[a * ne + b].at[j],
                            xs.at[pl.ds(row, rows), pl.ds(col, width)],
                            sem.at[(a * ne + b) * nz + j],
                        )
                    )
        for c in copies:
            c.start()
        for c in copies:
            c.wait()

    @pl.when(step < steps_t)
    def _():
        g = dot(xs[...], tg[0])
        u = dot(xs[...], tu[0])
        w = w_ref[...]
        a = g * jax.nn.sigmoid(g) * u
        at_ref[...] = jnp.where(w != 0.0, -w * a, 0.0).astype(BF)

    @pl.when(step >= steps_t)
    def _():
        g = dot(xs[...], sg[...])
        u = dot(xs[...], su[...])
        s = jax.nn.sigmoid(g)
        f2 = g * s
        act_ref[...] = (f2 * u).astype(BF)
        f1_ref[...] = u * s * (1.0 + g * (1.0 - s))
        f2_ref[...] = f2


def up_call(sc, w_rows, t_gate, t_up, s_gate, s_up, pieces, dims):
    nd, ne, nz, rows, width = dims
    total, model = rows * nd * ne, width * nz
    ht, hs = t_gate.shape[2], s_gate.shape[1]
    bt, bs = tile_of(ht, 256), tile_of(hs, 256)
    nt, ns = ht // bt, hs // bs
    t_at = lambda i, sc: jnp.minimum(i, nt - 1)
    s_at = lambda i, sc: jnp.maximum(i - nt, 0)
    return pl.pallas_call(
        functools.partial(up_kernel, nd, ne, nz, rows, width, nt),
        grid_spec=pltpu.PrefetchScalarGridSpec(
            num_scalar_prefetch=1,
            grid=(nt + ns,),
            in_specs=[
                pl.BlockSpec((total, 1), lambda i, sc: (0, 0)),
                pl.BlockSpec((1, model, bt), lambda i, sc: (0, 0, t_at(i, sc))),
                pl.BlockSpec((1, model, bt), lambda i, sc: (0, 0, t_at(i, sc))),
                pl.BlockSpec((model, bs), lambda i, sc: (0, s_at(i, sc))),
                pl.BlockSpec((model, bs), lambda i, sc: (0, s_at(i, sc))),
            ]
            + [ANY] * (nd * ne),
            out_specs=[
                pl.BlockSpec((total, bt), lambda i, sc: (0, t_at(i, sc))),
                pl.BlockSpec((total, bs), lambda i, sc: (0, s_at(i, sc))),
                pl.BlockSpec((total, bs), lambda i, sc: (0, s_at(i, sc))),
                pl.BlockSpec((total, bs), lambda i, sc: (0, s_at(i, sc))),
                pl.BlockSpec((total, model), lambda i, sc: (0, 0)),
            ],
            scratch_shapes=[pltpu.SemaphoreType.DMA((nd * ne * nz,))],
        ),
        out_shape=[
            jax.ShapeDtypeStruct((total, ht), BF),
            jax.ShapeDtypeStruct((total, hs), BF),
            jax.ShapeDtypeStruct((total, hs), F32),
            jax.ShapeDtypeStruct((total, hs), F32),
            jax.ShapeDtypeStruct((total, model), BF),
        ],
        compiler_params=params(),
        cost_estimate=cost(4 * total * model * (ht + hs), 4 * model * (ht + hs)),
        name="up",
    )(sc, w_rows, t_gate, t_up, s_gate, s_up, *pieces)


def down_kernel(with_student, sc, at, act, td, sd, out):
    p = dot(at[...], td[0])
    if with_student:
        p = p + dot(act[...], sd[...])
    out[...] = p.astype(BF)


def down_call(sc, at, act, t_down, s_down, nd, with_student):
    total, ht = at.shape
    hs, model = s_down.shape
    half = model // nd
    bn = tile_of(half, 512)
    n = half // bn
    return pl.pallas_call(
        functools.partial(down_kernel, with_student),
        grid_spec=pltpu.PrefetchScalarGridSpec(
            num_scalar_prefetch=1,
            grid=(n,),
            in_specs=[
                pl.BlockSpec((total, ht), lambda i, sc: (0, 0)),
                pl.BlockSpec((total, hs), lambda i, sc: (0, 0)),
                pl.BlockSpec((1, ht, bn), lambda i, sc: (0, 0, sc[0] * n + i)),
                pl.BlockSpec((hs, bn), lambda i, sc: (0, sc[0] * n + i))
                if with_student
                else ANY,
            ],
            out_specs=pl.BlockSpec((total, bn), lambda i, sc: (0, i)),
        ),
        out_shape=jax.ShapeDtypeStruct((total, half), BF),
        compiler_params=params(),
        cost_estimate=cost(2 * total * half * (ht + hs), 2 * half * (ht + hs)),
        name="down",
    )(sc, at, act, t_down, s_down)


def back_kernel(ne, last, n, model_tokens, grad_scale, sc, act, sd, *rest):
    blocks = rest[:ne]
    if last:
        dact_in, sq_in, f1, f2, gd_in, gd, dgp, dup, loss, acc, sq, act_t = rest[ne:]
    else:
        gd, acc, sq, act_t = rest[ne:]
    step = pl.program_id(0)

    @pl.when(step == 0)
    def _():
        act_t[...] = act[...].T
        if last:
            acc[...] = dact_in[...]
        else:
            acc[...] = jnp.zeros_like(acc)
        sq[...] = jnp.zeros_like(sq)

    d = jnp.concatenate([b[...] for b in blocks], axis=0)
    acc[...] += lax.dot_general(d, sd[...], (((1,), (1,)), ((), ())), preferred_element_type=F32)
    gd[...] = dot(act_t[...], d).astype(BF)
    f = d.astype(F32)
    s = sq[...]
    for k in range(d.shape[1] // 128):
        part = f[:, k * 128 : (k + 1) * 128]
        s = s + part * part
    sq[...] = s

    if last:

        @pl.when(step == n - 1)
        def _():
            dact = acc[...]
            dgp[...] = (dact * f1[...]).astype(BF)
            dup[...] = (dact * f2[...]).astype(BF)
            rb = sq.shape[0] // ne
            first = sc[0] == 1
            tot = jnp.zeros((rb, 128), F32)
            for e in range(ne):
                row = pl.multiple_of((sc[1] ^ e) * rb, rb)
                tot = tot + jnp.where(first, sq_in[pl.ds(row, rb), :], sq[pl.ds(row, rb), :])
            for e in range(ne):
                row = pl.multiple_of((sc[1] ^ e) * rb, rb)
                tot = tot + jnp.where(first, sq[pl.ds(row, rb), :], sq_in[pl.ds(row, rb), :])
            value = jnp.sum(jnp.sum(tot, axis=0, keepdims=True), axis=1, keepdims=True)
            loss[...] = value * (1.0 / (grad_scale * grad_scale)) / model_tokens


def back_call(sc, act, s_down, blocks, nd, carry, model_tokens, grad_scale):
    total, hs = act.shape
    model = s_down.shape[1]
    half = model // nd
    ne = len(blocks)
    rb = total // ne
    bn = tile_of(half, 512)
    n = half // bn
    last = carry is not None
    whole = lambda i, sc: (0, 0)
    col = lambda i, sc: (0, sc[0] * n + i)
    in_specs = [
        pl.BlockSpec((total, hs), whole),
        pl.BlockSpec((hs, bn), col),
    ] + [pl.BlockSpec((rb, bn), lambda i, sc: (0, i))] * ne
    args = [sc, act, s_down, *blocks]
    gd_shape = jax.ShapeDtypeStruct((hs, model), BF)
    if last:
        dact, sq, f1, f2, gd = carry
        in_specs += [
            pl.BlockSpec((total, hs), whole),
            pl.BlockSpec((total, 128), whole),
            pl.BlockSpec((total, hs), whole),
            pl.BlockSpec((total, hs), whole),
            ANY,
        ]
        args += [dact, sq, f1, f2, gd]
        out_specs = [
            pl.BlockSpec((hs, bn), col),
            pl.BlockSpec((total, hs), whole),
            pl.BlockSpec((total, hs), whole),
            pl.BlockSpec((1, 1), whole),
        ]
        out_shape = [
            gd_shape,
            jax.ShapeDtypeStruct((total, hs), BF),
            jax.ShapeDtypeStruct((total, hs), BF),
            jax.ShapeDtypeStruct((1, 1), F32),
        ]
        scratch = [
            pltpu.VMEM((total, hs), F32),
            pltpu.VMEM((total, 128), F32),
            pltpu.VMEM((hs, total), BF),
        ]
        aliases = {len(args) - 1: 0}
    else:
        out_specs = [
            pl.BlockSpec((hs, bn), col),
            pl.BlockSpec((total, hs), whole),
            pl.BlockSpec((total, 128), whole),
        ]
        out_shape = [
            gd_shape,
            jax.ShapeDtypeStruct((total, hs), F32),
            jax.ShapeDtypeStruct((total, 128), F32),
        ]
        scratch = [pltpu.VMEM((hs, total), BF)]
        aliases = {}
    return pl.pallas_call(
        functools.partial(back_kernel, ne, last, n, model_tokens, grad_scale),
        grid_spec=pltpu.PrefetchScalarGridSpec(
            num_scalar_prefetch=1,
            grid=(n,),
            in_specs=in_specs,
            out_specs=out_specs,
            scratch_shapes=scratch,
        ),
        out_shape=out_shape,
        input_output_aliases=aliases,
        compiler_params=params(),
        cost_estimate=cost(4 * total * half * hs, 4 * half * hs),
        name="back",
    )(*args)


def grad_kernel(xs, dgp, dup, gg, gu):
    x = xs[...]
    dims = (((0,), (0,)), ((), ()))
    gg[...] = lax.dot_general(x, dgp[...], dims, preferred_element_type=F32).astype(BF)
    gu[...] = lax.dot_general(x, dup[...], dims, preferred_element_type=F32).astype(BF)


def grad_call(xs, dgp, dup):
    total, model = xs.shape
    hs = dgp.shape[1]
    bn = tile_of(model, 512)
    whole = lambda i: (0, 0)
    return pl.pallas_call(
        grad_kernel,
        grid=(model // bn,),
        in_specs=[
            pl.BlockSpec((total, bn), lambda i: (0, i)),
            pl.BlockSpec((total, hs), whole),
            pl.BlockSpec((total, hs), whole),
        ],
        out_specs=[pl.BlockSpec((bn, hs), lambda i: (i, 0))] * 2,
        out_shape=[jax.ShapeDtypeStruct((model, hs), BF)] * 2,
        compiler_params=params(),
        cost_estimate=cost(4 * total * model * hs, 4 * model * hs),
        name="grad",
    )(xs, dgp, dup)


def body(tokens, expert_ids, gate_weights, t_gate, t_up, t_down, s_gate, s_up, s_down):
    nd, ne, nz = lax.axis_size("dp"), lax.axis_size("expert"), lax.axis_size("tensor")
    dp, ex, tz = lax.axis_index("dp"), lax.axis_index("expert"), lax.axis_index("tensor")
    rows, width = tokens.shape
    model = width * nz
    total = rows * ne * nd
    sc = jnp.stack([dp, ex, tz]).astype(jnp.int32)

    share = gate_weights / jnp.sum(gate_weights, axis=1, keepdims=True)
    names = expert_ids[:, :, None] == jnp.arange(ne, dtype=jnp.int32)[None, None, :]
    mix = jnp.sum(jnp.where(names, share[:, :, None], 0.0), axis=1)
    other = swap(mix, "dp", nd, 1)
    pair = jnp.where(dp == 0, jnp.stack([mix, other]), jnp.stack([other, mix]))
    mixes = [pair] + [swap(pair, "expert", ne, b) for b in range(1, ne)]
    w_all = jnp.stack(mixes).reshape(total, ne)
    own = jnp.arange(ne, dtype=jnp.int32)[None, :] == ex
    w_rows = jnp.sum(jnp.where(own, w_all, 0.0), axis=1, keepdims=True)

    zs = jnp.stack([tokens] + [swap(tokens, "tensor", nz, j) for j in range(1, nz)])
    xy = [zs] + [swap(zs, "expert", ne, b) for b in range(1, ne)]
    far = [swap(x, "dp", nd, 1) for x in xy]
    at, act, f1, f2, xs = up_call(
        sc, w_rows, t_gate, t_up, s_gate, s_up, xy + far, (nd, ne, nz, rows, width)
    )

    mine, theirs = dp[None].astype(jnp.int32), (1 - dp)[None].astype(jnp.int32)
    sent = down_call(theirs, at, act, t_down, s_down, nd, False)
    kept = down_call(mine, at, act, t_down, s_down, nd, True)
    got = swap(sent, "dp", nd, 1)
    half = model // nd
    rb = total // ne
    q = [
        (
            kept[b * rb : (b + 1) * rb].astype(F32) + got[b * rb : (b + 1) * rb].astype(F32)
        ).astype(BF)
        for b in range(ne)
    ]
    parts = [q[0]] + [swap(q[b], "expert", ne, b) for b in range(1, ne)]
    r = sum(p.astype(F32) for p in parts).astype(BF).reshape(nz, rb // nz, half)
    piece = lambda j: lax.dynamic_index_in_dim(r, tz ^ j, 0, keepdims=False)
    pieces = [piece(0)] + [swap(piece(j), "tensor", nz, j) for j in range(1, nz)]
    diff = sum(p.astype(F32) for p in pieces)
    grad_scale = 1.0 / math.sqrt(total)
    d_out = (diff * grad_scale).astype(BF)

    dz = [d_out] + [swap(d_out, "tensor", nz, j) for j in range(1, nz)]
    block = jnp.zeros((nz, rb // nz, half), BF)
    for j in range(nz):
        block = lax.dynamic_update_index_in_dim(block, dz[j], tz ^ j, 0)
    block = block.reshape(rb, half)
    near = [block] + [swap(block, "expert", ne, b) for b in range(1, ne)]
    far = [swap(x, "dp", nd, 1) for x in near]
    back = functools.partial(back_call, nd=nd, model_tokens=total * model, grad_scale=grad_scale)
    gd, dact, sq = back(jnp.stack([dp, ex]).astype(jnp.int32), act, s_down, near, carry=None)
    gd, dgp, dup, loss = back(
        jnp.stack([1 - dp, ex]).astype(jnp.int32), act, s_down, far, carry=(dact, sq, f1, f2, gd)
    )
    gg, gu = grad_call(xs, dgp, dup)
    return gg, gu, gd, loss[0, 0]


def solution(mesh):
    return jax.shard_map(
        body,
        mesh=mesh,
        in_specs=(
            P(("dp", "expert"), "tensor"),
            P(("dp", "expert"), None),
            P(("dp", "expert"), None),
            P("expert", None, ("dp", "tensor")),
            P("expert", None, ("dp", "tensor")),
            P("expert", ("dp", "tensor"), None),
            P(None, ("expert", "tensor")),
            P(None, ("expert", "tensor")),
            P(("expert", "tensor"), None),
        ),
        out_specs=(
            P(None, ("expert", "tensor")),
            P(None, ("expert", "tensor")),
            P(("expert", "tensor"), None),
            P(),
        ),
        check_vma=False,
    )
```

```python
import functools
import math

import jax
import jax.numpy as jnp
from jax import lax
from jax.experimental import pallas as pl
from jax.experimental.pallas import tpu as pltpu
from jax.sharding import PartitionSpec as P


BF = jnp.bfloat16
F32 = jnp.float32
ANY = pl.BlockSpec(memory_space=pl.ANY)
HBM = pl.BlockSpec(memory_space=pltpu.HBM)
VM = pl.BlockSpec(memory_space=pltpu.VMEM)
SM = pl.BlockSpec(memory_space=pltpu.SMEM)
MIB = 1024 * 1024
CHUNKS = 2


def swap(x, axis, n, r):
    return lax.ppermute(x, axis, [(i, i ^ r) for i in range(n)])


def tile_of(n, most):
    t = min(n, most)
    while n % t:
        t //= 2
    return t


def call(kernel, out_shape, in_specs, args, flops=0, moved=0, scratch=(), limit=4, out_specs=None):
    return pl.pallas_call(
        kernel,
        out_shape=out_shape,
        in_specs=in_specs,
        out_specs=jax.tree.map(lambda _: VM, out_shape) if out_specs is None else out_specs,
        scratch_shapes=list(scratch),
        compiler_params=pltpu.CompilerParams(vmem_limit_bytes=limit * MIB),
        cost_estimate=pl.CostEstimate(
            flops=int(flops), bytes_accessed=int(moved), transcendentals=0
        ),
    )(*args)


def shape(dims, dtype=BF):
    return jax.ShapeDtypeStruct(tuple(dims), dtype)


def dot(a, b):
    return jnp.dot(a, b, preferred_element_type=F32)


def whole(ref):
    return ref[...].astype(F32)


def pack_kernel(ne, sc, tokens, ids, gates, out):
    width = tokens.shape[1]
    out[:, :width] = tokens[...]
    g = gates[...]
    share = g / jnp.sum(g, axis=1, keepdims=True)
    lanes = lax.broadcasted_iota(jnp.int32, (tokens.shape[0], 128), 1)
    w = jnp.zeros(lanes.shape, F32)
    for k in range(ids.shape[1]):
        w = w + jnp.where(ids[:, k : k + 1] == lanes % ne, share[:, k : k + 1], 0.0)
    high = w.astype(BF).astype(F32)
    middle = (w - high).astype(BF).astype(F32)
    low = w - high - middle
    terms = jnp.where(lanes < ne, high, jnp.where(lanes < 2 * ne, middle, low))
    out[:, width:] = jnp.where(lanes < 3 * ne, terms, 0.0).astype(BF)


def pack(sc, tokens, ids, gates, ne):
    rows, width = tokens.shape
    return call(
        functools.partial(pack_kernel, ne),
        shape((rows, width + 128)),
        [SM] + [VM] * 3,
        (sc, tokens, ids, gates),
        moved=4 * rows * width,
    )


def stack_kernel(*refs):
    out, n = refs[-1], refs[0].shape[0]
    for i, r in enumerate(refs[:-1]):
        out[i * n : (i + 1) * n] = r[...]


def stack(xs):
    n, width = xs[0].shape
    return call(
        stack_kernel, shape((n * len(xs), width)), [VM] * len(xs), xs, moved=4 * len(xs) * n * width
    )


def up_kernel(nd, ne, nz, rows, width, sc, tg, tu, sg, su, *rest):
    count = nd * ne
    own, line = rest[:count], rest[count : 2 * count]
    at_ref, act_ref, f1_ref, f2_ref, xs_out = rest[2 * count : 2 * count + 5]
    xs, w_ref, tbuf, sbuf, sem, tsem, ssem, wsem, xsem = rest[2 * count + 5 :]
    bt, bs = tbuf.shape[3], sbuf.shape[4]
    nt, ns = tg.shape[2] // bt, sg.shape[1] // bs

    def teacher(i, slot):
        cols = pl.ds(pl.multiple_of(i * bt, bt), bt)
        return [
            pltpu.make_async_copy(w.at[0, :, cols], tbuf.at[slot, k], tsem.at[slot, k])
            for k, w in enumerate((tg, tu))
        ]

    def student(i):
        cols = pl.ds(pl.multiple_of(i * bs, bs), bs)
        return [
            pltpu.make_async_copy(w.at[:, cols], sbuf.at[i, k, 0], ssem.at[i, k])
            for k, w in enumerate((sg, su))
        ]

    def row_of(n):
        return pl.multiple_of((n % ne * nd + (sc[0] ^ (n // ne))) * rows, rows)

    copies = []
    for n in range(count):
        for j in range(nz):
            col = pl.multiple_of((sc[2] ^ j) * width, 128)
            src = line[n].at[pl.ds((j - 1) * rows, rows), :] if j else own[n].at[:, pl.ds(0, width)]
            dst = xs.at[pl.ds(row_of(n), rows), pl.ds(col, width)]
            copies.append(pltpu.make_async_copy(src, dst, sem.at[n * nz + j]))
    tails = [
        pltpu.make_async_copy(own[n].at[:, pl.ds(width, 128)], w_ref.at[n], wsem.at[n])
        for n in range(count)
    ]
    for c in teacher(0, 0) + tails + copies:
        c.start()
    for i in range(ns):
        for c in student(i):
            c.start()
    for c in tails + copies:
        c.wait()
    keep = pltpu.make_async_copy(xs, xs_out, xsem)
    keep.start()

    weights = []
    for b in range(ne):
        pair = []
        for a in range(nd):
            m = w_ref[a * ne + b].astype(F32)
            lanes = lax.broadcasted_iota(jnp.int32, m.shape, 1)
            ours = (lanes % ne == sc[1]) & (lanes < 3 * ne)
            pair.append(jnp.sum(jnp.where(ours, m, 0.0), axis=1, keepdims=True))
        for d in range(nd):
            value = pair[0]
            for a in range(1, nd):
                value = jnp.where((sc[0] ^ a) == d, pair[a], value)
            weights.append(value)
    w = jnp.concatenate(weights, axis=0)

    @pl.loop(0, nt)
    def _(i):
        slot = lax.rem(i, 2)

        @pl.when(i + 1 < nt)
        def _():
            for c in teacher(i + 1, 1 - slot):
                c.start()

        for c in teacher(i, slot):
            c.wait()
        at = pl.ds(pl.multiple_of(i * bt, bt), bt)
        g = dot(xs[...], tbuf[slot, 0])
        u = dot(xs[...], tbuf[slot, 1])
        a = g * jax.nn.sigmoid(g) * u
        at_ref[:, at] = jnp.where(w != 0.0, -w * a, 0.0).astype(BF)

    @pl.loop(0, ns)
    def _(i):
        for c in student(i):
            c.wait()
        at = pl.ds(pl.multiple_of(i * bs, bs), bs)
        g = dot(xs[...], sbuf[i, 0, 0])
        u = dot(xs[...], sbuf[i, 1, 0])
        s = jax.nn.sigmoid(g)
        f2 = g * s
        act_ref[:, at] = (f2 * u).astype(BF)
        f1_ref[:, at] = u * s * (1.0 + g * (1.0 - s))
        f2_ref[:, at] = f2

    keep.wait()


def up(sc, tg, tu, sg, su, own, line, dims):
    nd, ne, nz, rows, width = dims
    total, model = rows * nd * ne, width * nz
    ht, hs = tg.shape[2], sg.shape[1]
    bt, bs = tile_of(ht, 256), tile_of(hs, 256)
    count = nd * ne
    return call(
        functools.partial(up_kernel, nd, ne, nz, rows, width),
        [
            shape((total, ht)),
            shape((total, hs)),
            shape((total, hs), F32),
            shape((total, hs), F32),
            shape((total, model)),
        ],
        [SM] + [ANY] * (4 + 2 * count),
        (sc, tg, tu, sg, su, *own, *line),
        flops=4 * total * model * (ht + hs),
        moved=4 * model * (ht + hs),
        scratch=[
            pltpu.VMEM((total, model), BF),
            pltpu.VMEM((count, rows, 128), BF),
            pltpu.VMEM((2, 2, model, bt), BF),
            pltpu.VMEM((hs // bs, 2, 1, model, bs), BF),
            pltpu.SemaphoreType.DMA((count * nz,)),
            pltpu.SemaphoreType.DMA((2, 2)),
            pltpu.SemaphoreType.DMA((hs // bs, 2)),
            pltpu.SemaphoreType.DMA((count,)),
            pltpu.SemaphoreType.DMA,
        ],
        out_specs=[VM, VM, VM, VM, HBM],
        limit=28,
    )


def down_kernel(kept, chunk, chunks, nd, ne, *refs):
    if kept:
        sc, at, act, td, sd, got = refs[:6]
        outs, scratch = refs[6 : 6 + ne], refs[6 + ne :]
    else:
        sc, at, td = refs[:3]
        outs, scratch = refs[3:4], refs[4:]
    model = td.shape[2]
    width = model // nd // chunks
    bn = tile_of(width, 640)
    base = (sc[0] if kept else 1 - sc[0]) * (model // nd) + chunk * width
    tbuf, tsem = scratch[:2]
    n = width // bn

    def fetch(i):
        cols = pl.ds(pl.multiple_of(base + i * bn, 128), bn)
        copies = [pltpu.make_async_copy(td.at[0, :, cols], tbuf.at[i], tsem.at[i])]
        if kept:
            sbuf, ssem = scratch[2:]
            copies.append(pltpu.make_async_copy(sd.at[:, cols], sbuf.at[i], ssem.at[i]))
        return copies

    for i in range(n):
        for c in fetch(i):
            c.start()
    for i in range(n):
        for c in fetch(i):
            c.wait()
        p = dot(at[...], tbuf[i])
        here = slice(i * bn, (i + 1) * bn)
        if kept:
            p = p + dot(act[...], scratch[2][i]) + got[:, here].astype(F32)
            rb = p.shape[0] // ne
            for b in range(ne):
                outs[b][:, here] = p[b * rb : (b + 1) * rb].astype(BF)
        else:
            outs[0][:, here] = p.astype(BF)


def down(sc, at, act, td, sd, got, chunk, nd, ne):
    kept = got is not None
    total, ht = at.shape
    hs, model = sd.shape
    width = model // nd // CHUNKS
    bn = tile_of(width, 640)
    n = width // bn
    scratch = [pltpu.VMEM((n, ht, bn), BF), pltpu.SemaphoreType.DMA((n,))]
    if kept:
        scratch += [pltpu.VMEM((n, hs, bn), BF), pltpu.SemaphoreType.DMA((n,))]
        args, specs = (sc, at, act, td, sd, got), [SM, VM, VM, ANY, ANY, VM]
        out = [shape((total // ne, width))] * ne
    else:
        args, specs = (sc, at, td), [SM, VM, ANY]
        out = [shape((total, width))]
    return call(
        functools.partial(down_kernel, kept, chunk, CHUNKS, nd, ne),
        out,
        specs,
        args,
        flops=2 * total * width * (ht + (hs if kept else 0)),
        moved=2 * width * (ht + (hs if kept else 0)),
        scratch=scratch,
        limit=10,
    )


def sum_kernel(nz, count, sc, *refs):
    parts, outs = refs[:count], refs[count:]
    rp = outs[0].shape[0]
    for j in range(nz):
        rows = pl.ds(pl.multiple_of((sc[2] ^ j) * rp, rp), rp)
        outs[j][...] = sum(p[rows, :].astype(F32) for p in parts).astype(BF)


def sum_parts(sc, parts, nz):
    rb, width = parts[0].shape
    return call(
        functools.partial(sum_kernel, nz, len(parts)),
        [shape((rb // nz, width))] * nz,
        [SM] + [VM] * len(parts),
        (sc, *parts),
        moved=4 * len(parts) * rb * width,
    )


def final_kernel(chunks, scale, *refs):
    parts, out = refs[:-1], refs[-1]
    count = len(parts) // chunks
    width = parts[0].shape[1]
    for c in range(chunks):
        total = sum(whole(p) for p in parts[c * count : (c + 1) * count])
        out[:, c * width : (c + 1) * width] = (total * scale).astype(BF)


def final(parts, scale):
    rp, width = parts[0][0].shape
    flat = [p for line in parts for p in line]
    return call(
        functools.partial(final_kernel, len(parts), scale),
        shape((rp, width * len(parts))),
        [VM] * len(flat),
        flat,
        moved=4 * len(flat) * rp * width,
    )


def back_kernel(nd, ne, nz, model_tokens, grad_scale, sc, act, sd, f1, f2, *rest):
    count = nd * ne
    own, line = rest[:count], rest[count : 2 * count]
    gd, dgp, dup, loss, d_ref, act_t, sq, gbuf, sem, gsem = rest[2 * count :]
    rp, half = own[0].shape
    total, hs = act.shape
    model = half * nd
    rb = total // ne

    copies = []
    for n in range(count):
        for j in range(nz):
            row = pl.multiple_of(n % ne * rb + (sc[2] ^ j) * rp, rp)
            col = pl.multiple_of((sc[0] ^ (n // ne)) * half, 128)
            src = line[n].at[pl.ds((j - 1) * rp, rp), :] if j else own[n]
            dst = d_ref.at[pl.ds(row, rp), pl.ds(col, half)]
            copies.append(pltpu.make_async_copy(src, dst, sem.at[n * nz + j]))
    for c in copies:
        c.start()
    act_t[...] = act[...].T
    for c in copies:
        c.wait()
    bn = tile_of(model, 1280)
    n = model // bn
    dact = jnp.zeros((total, hs), F32)
    for i in range(n):
        cols = slice(i * bn, (i + 1) * bn)
        dact = dact + lax.dot_general(
            d_ref[:, cols], sd[:, cols], (((1,), (1,)), ((), ())), preferred_element_type=F32
        )
    dgp[...] = (dact * f1[...]).astype(BF)
    dup[...] = (dact * f2[...]).astype(BF)
    s = jnp.zeros((total, 128), F32)
    out = [
        pltpu.make_async_copy(gbuf.at[i], gd.at[:, i * bn : (i + 1) * bn], gsem.at[i])
        for i in range(n)
    ]
    for i in range(n):
        d = d_ref[:, i * bn : (i + 1) * bn]
        gbuf[i] = dot(act_t[...], d).astype(BF)
        out[i].start()
        f = d.astype(F32)
        for k in range(bn // 128):
            part = f[:, k * 128 : (k + 1) * 128]
            s = s + part * part
    sq[...] = s
    tot = jnp.zeros((rb, 128), F32)
    for e in range(ne):
        tot = tot + sq[pl.ds(pl.multiple_of((sc[1] ^ e) * rb, rb), rb), :]
    value = jnp.sum(jnp.sum(tot, axis=0, keepdims=True), axis=1, keepdims=True)
    loss[...] = value * (1.0 / (grad_scale * grad_scale)) / model_tokens
    for c in out:
        c.wait()


def back(sc, act, sd, f1, f2, own, line, dims, model_tokens, grad_scale):
    nd, ne, nz = dims
    total, hs = act.shape
    model = sd.shape[1]
    bn = tile_of(model, 1280)
    n = model // bn
    return call(
        functools.partial(back_kernel, nd, ne, nz, model_tokens, grad_scale),
        [shape((hs, model)), shape((total, hs)), shape((total, hs)), shape((1, 1), F32)],
        [SM] + [VM] * 4 + [ANY] * (2 * nd * ne),
        (sc, act, sd, f1, f2, *own, *line),
        flops=4 * total * model * hs,
        moved=2 * model * hs,
        scratch=[
            pltpu.VMEM((total, model), BF),
            pltpu.VMEM((hs, total), BF),
            pltpu.VMEM((total, 128), F32),
            pltpu.VMEM((n, hs, bn), BF),
            pltpu.SemaphoreType.DMA((nd * ne * nz,)),
            pltpu.SemaphoreType.DMA((n,)),
        ],
        out_specs=[HBM, VM, VM, VM],
        limit=20,
    )


def grad_kernel(xs, dgp, dup, gg, gu, buf, sem):
    model = xs.shape[1]
    bn = tile_of(model, 1280)
    dims = (((0,), (0,)), ((), ()))
    out = []
    for i in range(model // bn):
        rows = slice(i * bn, (i + 1) * bn)
        for k, (d, g) in enumerate(((dgp, gg), (dup, gu))):
            n = 2 * i + k
            buf[n] = lax.dot_general(
                xs[:, rows], d[...], dims, preferred_element_type=F32
            ).astype(BF)
            out.append(pltpu.make_async_copy(buf.at[n], g.at[rows, :], sem.at[n]))
            out[-1].start()
    for c in out:
        c.wait()


def grad(xs, dgp, dup):
    total, model = xs.shape
    hs = dgp.shape[1]
    bn = tile_of(model, 1280)
    n = 2 * (model // bn)
    return call(
        grad_kernel,
        [shape((model, hs))] * 2,
        [VM] * 3,
        (xs, dgp, dup),
        flops=4 * total * model * hs,
        moved=4 * model * hs,
        scratch=[pltpu.VMEM((n, bn, hs), BF), pltpu.SemaphoreType.DMA((n,))],
        out_specs=[HBM] * 2,
        limit=24,
    )


def body(tokens, expert_ids, gate_weights, t_gate, t_up, t_down, s_gate, s_up, s_down):
    nd, ne, nz = lax.axis_size("dp"), lax.axis_size("expert"), lax.axis_size("tensor")
    rows, width = tokens.shape
    model = width * nz
    total = rows * ne * nd
    sc = jnp.stack(
        [lax.axis_index("dp"), lax.axis_index("expert"), lax.axis_index("tensor")]
    ).astype(jnp.int32)

    def spread(x, packed):
        line = [swap(x, "tensor", nz, j) for j in range(1, nz)]
        own = [packed] + [swap(packed, "expert", ne, b) for b in range(1, ne)]
        line = stack(line)
        lines = [line] + [swap(line, "expert", ne, b) for b in range(1, ne)]
        far = lambda xs: xs + [swap(z, "dp", nd, 1) for z in xs]
        return far(own), far(lines)

    own, lines = spread(tokens, pack(sc, tokens, expert_ids, gate_weights, ne))
    at, act, f1, f2, xs = up(
        sc, t_gate, t_up, s_gate, s_up, own, lines, (nd, ne, nz, rows, width)
    )

    sent = [down(sc, at, act, t_down, s_down, None, c, nd, ne)[0] for c in range(CHUNKS)]
    got = [swap(s, "dp", nd, 1) for s in sent]
    last = []
    for c in range(CHUNKS):
        kept = down(sc, at, act, t_down, s_down, got[c], c, nd, ne)
        parts = [kept[0]] + [swap(kept[b], "expert", ne, b) for b in range(1, ne)]
        own = sum_parts(sc, parts, nz)
        last.append([own[0]] + [swap(own[j], "tensor", nz, j) for j in range(1, nz)])
    grad_scale = 1.0 / math.sqrt(total)
    d_out = final(last, grad_scale)

    own, lines = spread(d_out, d_out)
    gd, dgp, dup, loss = back(
        sc, act, s_down, f1, f2, own, lines, (nd, ne, nz), total * model, grad_scale
    )
    gg, gu = grad(xs, dgp, dup)
    return gg, gu, gd, loss[0, 0]


def solution(mesh):
    return jax.shard_map(
        body,
        mesh=mesh,
        in_specs=(
            P(("dp", "expert"), "tensor"),
            P(("dp", "expert"), None),
            P(("dp", "expert"), None),
            P("expert", None, ("dp", "tensor")),
            P("expert", None, ("dp", "tensor")),
            P("expert", ("dp", "tensor"), None),
            P(None, ("expert", "tensor")),
            P(None, ("expert", "tensor")),
            P(("expert", "tensor"), None),
        ),
        out_specs=(
            P(None, ("expert", "tensor")),
            P(None, ("expert", "tensor")),
            P(("expert", "tensor"), None),
            P(),
        ),
        check_vma=False,
    )
```

```python
import functools
import math

import jax
import jax.numpy as jnp
from jax import lax
from jax.experimental import pallas as pl
from jax.experimental.pallas import tpu as pltpu
from jax.sharding import PartitionSpec as P


BF = jnp.bfloat16
F32 = jnp.float32
ANY = pl.BlockSpec(memory_space=pl.ANY)
HBM = pl.BlockSpec(memory_space=pltpu.HBM)
VM = pl.BlockSpec(memory_space=pltpu.VMEM)
SM = pl.BlockSpec(memory_space=pltpu.SMEM)
MIB = 1024 * 1024


def swap(x, axis, n, r):
    return lax.ppermute(x, axis, [(i, i ^ r) for i in range(n)])


def tile_of(n, most):
    t = min(n, most)
    while n % t:
        t //= 2
    return t


def even(n):
    return max(k for k in range(128, 641, 128) if n % k == 0)


def call(kernel, out_shape, in_specs, args, flops=0, moved=0, scratch=(), limit=4, out_specs=None):
    return pl.pallas_call(
        kernel,
        out_shape=out_shape,
        in_specs=in_specs,
        out_specs=jax.tree.map(lambda _: VM, out_shape) if out_specs is None else out_specs,
        scratch_shapes=list(scratch),
        compiler_params=pltpu.CompilerParams(vmem_limit_bytes=limit * MIB),
        cost_estimate=pl.CostEstimate(
            flops=int(flops), bytes_accessed=int(moved), transcendentals=0
        ),
    )(*args)


def shape(dims, dtype=BF):
    return jax.ShapeDtypeStruct(tuple(dims), dtype)


def dot(a, b):
    return jnp.dot(a, b, preferred_element_type=F32)


def whole(ref):
    return ref[...].astype(F32)


def pack_kernel(ne, sc, tokens, ids_in, gates_in, out, ids, gates, sem):
    rows, width = tokens.shape
    copies = [
        pltpu.make_async_copy(src, dst, sem.at[n])
        for n, (src, dst) in enumerate(
            ((ids_in, ids), (gates_in, gates), (tokens, out.at[:, pl.ds(0, width)]))
        )
    ]
    for c in copies:
        c.start()
    for c in copies:
        c.wait()
    g = gates[...]
    share = g / jnp.sum(g, axis=0, keepdims=True)
    lines = lax.broadcasted_iota(jnp.int32, (128, rows), 0)
    w = jnp.zeros(lines.shape, F32)
    for k in range(ids.shape[0]):
        w = w + jnp.where(ids[k : k + 1, :] == lines % ne, share[k : k + 1, :], 0.0)
    high = w.astype(BF).astype(F32)
    middle = (w - high).astype(BF).astype(F32)
    low = w - high - middle
    terms = jnp.where(lines < ne, high, jnp.where(lines < 2 * ne, middle, low))
    terms = jnp.where(lines < 3 * ne, terms, 0.0)
    out[:, width:] = terms.T.astype(BF)


def pack(sc, tokens, ids, gates, ne):
    rows, width = tokens.shape
    return call(
        functools.partial(pack_kernel, ne),
        shape((rows, width + 128)),
        [SM, HBM, HBM, HBM],
        (sc, *map(in_hbm, (tokens, ids.T, gates.T))),
        moved=4 * rows * width,
        scratch=[
            pltpu.VMEM(ids.shape[::-1], jnp.int32),
            pltpu.VMEM(gates.shape[::-1], F32),
            pltpu.SemaphoreType.DMA((3,)),
        ],
    )


def in_hbm(x):
    return pltpu.with_memory_space_constraint(x, pltpu.HBM)


def load_kernel(*refs):
    n = (len(refs) - 2) // 2
    copies = [
        pltpu.make_async_copy(refs[1 + k], refs[1 + n + k], refs[-1].at[k]) for k in range(n)
    ]
    for c in copies:
        c.start()
    for c in copies:
        c.wait()


def load(after, weights):
    return call(
        load_kernel,
        [shape(w.shape) for w in weights],
        [ANY] + [HBM] * len(weights),
        (after, *map(in_hbm, weights)),
        moved=2 * sum(w.size for w in weights),
        scratch=[pltpu.SemaphoreType.DMA((len(weights),))],
        limit=1,
    )


def stack_kernel(*refs):
    out, n = refs[-1], refs[0].shape[0]
    for i, r in enumerate(refs[:-1]):
        out[i * n : (i + 1) * n] = r[...]


def stack(xs):
    n, width = xs[0].shape
    return call(
        stack_kernel, shape((n * len(xs), width)), [VM] * len(xs), xs, moved=4 * len(xs) * n * width
    )


def up_kernel(nd, ne, nz, rows, width, sc, tg, tu, sg_in, su_in, td_in, *rest):
    count = nd * ne
    own, line = rest[:count], rest[count : 2 * count]
    at_ref, act_ref, f1_ref, f2_ref, xs, td = rest[2 * count : 2 * count + 6]
    sg, su, w_ref, sem, wsem, dsem = rest[2 * count + 6 :]
    bt, bs = tile_of(tg.shape[2], 256), tile_of(sg.shape[1], 256)
    nt, ns = tg.shape[2] // bt, sg.shape[1] // bs

    def row_of(n):
        return pl.multiple_of((n % ne * nd + (sc[0] ^ (n // ne))) * rows, rows)

    copies = []
    for n in range(count):
        for j in range(nz):
            col = pl.multiple_of((sc[2] ^ j) * width, 128)
            src = line[n].at[pl.ds((j - 1) * rows, rows), :] if j else own[n].at[:, pl.ds(0, width)]
            dst = xs.at[pl.ds(row_of(n), rows), pl.ds(col, width)]
            copies.append(pltpu.make_async_copy(src, dst, sem.at[n * nz + j]))
    tails = [
        pltpu.make_async_copy(own[n].at[:, pl.ds(width, 128)], w_ref.at[n], wsem.at[n])
        for n in range(count)
    ]
    for c in tails + copies:
        c.start()
    for c in tails + copies:
        c.wait()
    ahead = [
        pltpu.make_async_copy(src, dst, dsem.at[k])
        for k, (src, dst) in enumerate(((sg_in, sg), (su_in, su), (td_in, td)))
    ]
    for c in ahead:
        c.start()

    weights = []
    for b in range(ne):
        pair = []
        for a in range(nd):
            m = w_ref[a * ne + b].astype(F32)
            lanes = lax.broadcasted_iota(jnp.int32, m.shape, 1)
            ours = (lanes % ne == sc[1]) & (lanes < 3 * ne)
            pair.append(jnp.sum(jnp.where(ours, m, 0.0), axis=1, keepdims=True))
        for d in range(nd):
            value = pair[0]
            for a in range(1, nd):
                value = jnp.where((sc[0] ^ a) == d, pair[a], value)
            weights.append(value)
    w = jnp.concatenate(weights, axis=0)

    cut = tile_of(nz * width, 1280)
    cuts = [slice(k, k + cut) for k in range(0, nz * width, cut)]

    @pl.loop(0, nt)
    def _(i):
        at = pl.ds(pl.multiple_of(i * bt, bt), bt)
        g = sum(dot(xs[:, k], tg[0, k, at]) for k in cuts)
        u = sum(dot(xs[:, k], tu[0, k, at]) for k in cuts)
        a = g * jax.nn.sigmoid(g) * u
        at_ref[:, at] = jnp.where(w != 0.0, -w * a, 0.0).astype(BF)

    for c in ahead[:2]:
        c.wait()

    @pl.loop(0, ns)
    def _(i):
        at = pl.ds(pl.multiple_of(i * bs, bs), bs)
        g = sum(dot(xs[:, k], sg[k, at]) for k in cuts)
        u = sum(dot(xs[:, k], su[k, at]) for k in cuts)
        s = jax.nn.sigmoid(g)
        f2 = g * s
        act_ref[:, at] = (f2 * u).astype(BF)
        f1_ref[:, at] = u * s * (1.0 + g * (1.0 - s))
        f2_ref[:, at] = f2

    for c in ahead[2:]:
        c.wait()


def up(sc, tg, tu, sg, su, td, own, line, dims):
    nd, ne, nz, rows, width = dims
    total, model = rows * nd * ne, width * nz
    ht, hs = tg.shape[2], sg.shape[1]
    count = nd * ne
    return call(
        functools.partial(up_kernel, nd, ne, nz, rows, width),
        [
            shape((total, ht)),
            shape((total, hs)),
            shape((total, hs), F32),
            shape((total, hs), F32),
            shape((total, model)),
            shape(td.shape),
        ],
        [SM] + [VM] * 2 + [HBM] * 3 + [ANY] * (2 * count),
        (sc, tg, tu, *map(in_hbm, (sg, su, td)), *own, *line),
        flops=4 * total * model * (ht + hs),
        moved=2 * total * model,
        scratch=[
            pltpu.VMEM(sg.shape, BF),
            pltpu.VMEM(su.shape, BF),
            pltpu.VMEM((count, rows, 128), BF),
            pltpu.SemaphoreType.DMA((count * nz,)),
            pltpu.SemaphoreType.DMA((count,)),
            pltpu.SemaphoreType.DMA((3,)),
        ],
        limit=15,
    )


def column(sc, other, base, model, nd, i, bn):
    half = model // nd
    start = ((1 - sc[0]) if other else sc[0]) * half + base
    return pl.ds(pl.multiple_of(start + i * bn, 128), bn)


def sent_kernel(base, nd, sc, at, td, *rest):
    out = rest[0]
    if len(rest) > 1:
        sd_in, out, sd, sem = rest
        ahead = pltpu.make_async_copy(sd_in, sd, sem)
        ahead.start()
    model, width = td.shape[2], out.shape[1]
    bn = even(width)
    for i in range(width // bn):
        cols = column(sc, True, base, model, nd, i, bn)
        out[:, i * bn : (i + 1) * bn] = dot(at[...], td[0, :, cols]).astype(BF)
    if len(rest) > 1:
        ahead.wait()


def sent_part(sc, at, td, base, width, nd, bring=()):
    total, ht = at.shape
    return call(
        functools.partial(sent_kernel, base, nd),
        [shape((total, width))] + [shape(w.shape) for w in bring],
        [SM, VM, VM] + [HBM] * len(bring),
        (sc, at, td, *map(in_hbm, bring)),
        flops=2 * total * width * ht,
        moved=2 * total * width,
        scratch=[pltpu.SemaphoreType.DMA] * len(bring),
        limit=4,
    )


def kept_kernel(base, nd, sc, at, act, td, sd, out):
    model, width = td.shape[2], out.shape[1]
    bn = even(width)
    for i in range(width // bn):
        cols = column(sc, False, base, model, nd, i, bn)
        out[:, i * bn : (i + 1) * bn] = dot(at[...], td[0, :, cols]) + dot(act[...], sd[:, cols])


def kept_part(sc, at, act, td, sd, base, width, nd):
    total, ht = at.shape
    hs = sd.shape[0]
    return call(
        functools.partial(kept_kernel, base, nd),
        shape((total, width), F32),
        [SM] + [VM] * 4,
        (sc, at, act, td, sd),
        flops=2 * total * width * (ht + hs),
        moved=2 * total * width,
        limit=4,
    )


def blocks_kernel(own, got, *outs):
    rb = outs[0].shape[0]
    for b, out in enumerate(outs):
        rows = slice(b * rb, (b + 1) * rb)
        out[...] = (own[rows] + got[rows].astype(F32)).astype(BF)


def blocks(own, got, ne):
    total, width = own.shape
    return call(
        blocks_kernel,
        [shape((total // ne, width))] * ne,
        [VM, VM],
        (own, got),
        moved=8 * total * width,
    )


def lines_kernel(ne, sc, own, got, *outs):
    nz = len(outs)
    rb = own.shape[0] // ne
    rp = rb // nz
    for j, out in enumerate(outs):
        for b in range(ne):
            rows = pl.ds(pl.multiple_of(b * rb + (sc[2] ^ j) * rp, rp), rp)
            out[b * rp : (b + 1) * rp] = (own[rows, :] + got[rows, :].astype(F32)).astype(BF)


def line_blocks(sc, own, got, ne, nz):
    total, width = own.shape
    return call(
        functools.partial(lines_kernel, ne),
        [shape((total // nz, width))] * nz,
        [SM, VM, VM],
        (sc, own, got),
        moved=8 * total * width,
    )


def sum_kernel(pick, count, sc, *refs):
    parts, outs = refs[:count], refs[count:]
    rp = outs[0].shape[0]
    for j, out in enumerate(outs):
        first = (sc[2] ^ j) * rp if pick else j * rp
        rows = pl.ds(pl.multiple_of(first, rp), rp)
        out[...] = sum(p[rows, :].astype(F32) for p in parts).astype(BF)


def sum_parts(sc, parts, n, pick):
    rb, width = parts[0].shape
    return call(
        functools.partial(sum_kernel, pick, len(parts)),
        [shape((rb // n, width))] * n,
        [SM] + [VM] * len(parts),
        (sc, *parts),
        moved=4 * len(parts) * rb * width,
    )


def final_kernel(counts, scale, *refs):
    out, at, col = refs[-1], 0, 0
    for n in counts:
        parts = refs[at : at + n]
        width = parts[0].shape[1]
        out[:, col : col + width] = (sum(whole(p) for p in parts) * scale).astype(BF)
        at, col = at + n, col + width


def final(groups, scale):
    rp = groups[0][0].shape[0]
    width = sum(g[0].shape[1] for g in groups)
    flat = [p for g in groups for p in g]
    return call(
        functools.partial(final_kernel, [len(g) for g in groups], scale),
        shape((rp, width)),
        [VM] * len(flat),
        flat,
        moved=8 * rp * width,
    )


def back_kernel(nd, ne, nz, model_tokens, grad_scale, sc, act, sd, f1, f2, x_in, *rest):
    count = nd * ne
    own, line = rest[:count], rest[count : 2 * count]
    gg, gu, gd, loss = rest[2 * count : 2 * count + 4]
    xs, d_ref, act_t, sq, dpre, dbuf, xbuf, xsem, sem, dsem, gsem = rest[2 * count + 4 :]
    rp, half = own[0].shape
    total, hs = act.shape
    model = half * nd
    rb = total // ne
    fetch = pltpu.make_async_copy(x_in, xs, xsem)
    fetch.start()
    copies = []
    for n in range(count):
        for j in range(nz):
            row = pl.multiple_of(n % ne * rb + (sc[2] ^ j) * rp, rp)
            col = pl.multiple_of((sc[0] ^ (n // ne)) * half, 128)
            src = line[n].at[pl.ds((j - 1) * rp, rp), :] if j else own[n]
            dst = d_ref.at[pl.ds(row, rp), pl.ds(col, half)]
            copies.append(pltpu.make_async_copy(src, dst, sem.at[n * nz + j]))
    for c in copies:
        c.start()
    act_t[...] = act[...].T
    for c in copies:
        c.wait()
    bn = dbuf.shape[2]
    n = model // bn
    dact = jnp.zeros((total, hs), F32)
    out = []
    s = jnp.zeros((total, 128), F32)
    for i in range(n):
        here = slice(i * bn, (i + 1) * bn)
        dbuf[i] = dot(act_t[...], d_ref[:, here]).astype(BF)
        out.append(pltpu.make_async_copy(dbuf.at[i], gd.at[:, here], dsem.at[i]))
        out[-1].start()
        dact = dact + lax.dot_general(
            d_ref[:, here], sd[:, here], (((1,), (1,)), ((), ())), preferred_element_type=F32
        )
        f = d_ref[:, here].astype(F32)
        for k in range(bn // 128):
            part = f[:, k * 128 : (k + 1) * 128]
            s = s + part * part
    dpre[:, :hs] = (dact * f1[...]).astype(BF)
    dpre[:, hs:] = (dact * f2[...]).astype(BF)
    fetch.wait()
    for i in range(n):
        here = slice(i * bn, (i + 1) * bn)
        both = lax.dot_general(
            xs[:, here], dpre[...], (((0,), (0,)), ((), ())), preferred_element_type=F32
        ).astype(BF)
        for k, g in enumerate((gg, gu)):
            at = 2 * i + k
            xbuf[at] = both[:, k * hs : (k + 1) * hs]
            out.append(pltpu.make_async_copy(xbuf.at[at], g.at[here, :], gsem.at[at]))
            out[-1].start()
    sq[...] = s
    tot = jnp.zeros((rb, 128), F32)
    for e in range(ne):
        tot = tot + sq[pl.ds(pl.multiple_of((sc[1] ^ e) * rb, rb), rb), :]
    value = jnp.sum(jnp.sum(tot, axis=0, keepdims=True), axis=1, keepdims=True)
    loss[...] = value * (1.0 / (grad_scale * grad_scale)) / model_tokens
    for c in out:
        c.wait()


def back(sc, act, sd, f1, f2, xs, own, line, dims, model_tokens, grad_scale):
    nd, ne, nz = dims
    total, hs = act.shape
    model = sd.shape[1]
    bn = tile_of(model, 1280)
    n = model // bn
    return call(
        functools.partial(back_kernel, nd, ne, nz, model_tokens, grad_scale),
        [shape((model, hs)), shape((model, hs)), shape((hs, model)), shape((1, 1), F32)],
        [SM] + [VM] * 4 + [ANY] * (1 + 2 * nd * ne),
        (sc, act, sd, f1, f2, xs, *own, *line),
        flops=8 * total * model * hs,
        moved=6 * model * hs,
        scratch=[
            pltpu.VMEM((total, model), BF),
            pltpu.VMEM((total, model), BF),
            pltpu.VMEM((hs, total), BF),
            pltpu.VMEM((total, 128), F32),
            pltpu.VMEM((total, 2 * hs), BF),
            pltpu.VMEM((n, hs, bn), BF),
            pltpu.VMEM((2 * n, bn, hs), BF),
            pltpu.SemaphoreType.DMA,
            pltpu.SemaphoreType.DMA((nd * ne * nz,)),
            pltpu.SemaphoreType.DMA((n,)),
            pltpu.SemaphoreType.DMA((2 * n,)),
        ],
        out_specs=[HBM, HBM, HBM, VM],
        limit=32,
    )


def body(tokens, expert_ids, gate_weights, t_gate, t_up, t_down, s_gate, s_up, s_down):
    nd, ne, nz = lax.axis_size("dp"), lax.axis_size("expert"), lax.axis_size("tensor")
    rows, width = tokens.shape
    model = width * nz
    total = rows * ne * nd
    sc = jnp.stack(
        [lax.axis_index("dp"), lax.axis_index("expert"), lax.axis_index("tensor")]
    ).astype(jnp.int32)

    def spread(x, packed):
        line = [swap(x, "tensor", nz, j) for j in range(1, nz)]
        own = [packed] + [swap(packed, "expert", ne, b) for b in range(1, ne)]
        line = stack(line)
        lines = [line] + [swap(line, "expert", ne, b) for b in range(1, ne)]
        own += [swap(z, "dp", nd, 1) for z in own]
        lines += [swap(z, "dp", nd, 1) for z in lines]
        return own, lines

    own, lines = spread(tokens, pack(sc, tokens, expert_ids, gate_weights, ne))
    loaded = []
    for w in (t_gate, t_up):
        loaded += load(lines[0], (w,))
    at, act, f1, f2, xs, td = up(
        sc, *loaded, s_gate, s_up, t_down, own, lines, (nd, ne, nz, rows, width)
    )

    half = model // nd
    cut = half - max(128, half // 10 // 128 * 128)
    parts = ((0, cut), (cut, half - cut))
    sent, sd = sent_part(sc, at, td, *parts[0], nd, [s_down])
    sent = [sent, *sent_part(sc, at, td, *parts[1], nd)]
    got = [swap(s, "dp", nd, 1) for s in sent]
    kept = [kept_part(sc, at, act, td, sd, *p, nd) for p in parts]

    def over(xs, axis, n):
        return [xs[0]] + [swap(xs[k], axis, n, k) for k in range(1, n)]

    wide = over(blocks(kept[0], got[0], ne), "expert", ne)
    slim = over(line_blocks(sc, kept[1], got[1], ne, nz), "tensor", nz)
    slim = over(sum_parts(sc, slim, ne, False), "expert", ne)
    wide = sum_parts(sc, wide, nz, True)
    wide = over(wide, "tensor", nz)
    grad_scale = 1.0 / math.sqrt(total)
    d_out = final((wide, slim), grad_scale)

    own, lines = spread(d_out, d_out)
    gg, gu, gd, loss = back(
        sc, act, sd, f1, f2, xs, own, lines, (nd, ne, nz), total * model, grad_scale
    )
    return gg, gu, gd, loss[0, 0]


def solution(mesh):
    return jax.shard_map(
        body,
        mesh=mesh,
        in_specs=(
            P(("dp", "expert"), "tensor"),
            P(("dp", "expert"), None),
            P(("dp", "expert"), None),
            P("expert", None, ("dp", "tensor")),
            P("expert", None, ("dp", "tensor")),
            P("expert", ("dp", "tensor"), None),
            P(None, ("expert", "tensor")),
            P(None, ("expert", "tensor")),
            P(("expert", "tensor"), None),
        ),
        out_specs=(
            P(None, ("expert", "tensor")),
            P(None, ("expert", "tensor")),
            P(("expert", "tensor"), None),
            P(),
        ),
        check_vma=False,
    )
```

```python
import functools
import math

import jax
import jax.numpy as jnp
from jax import lax
from jax.experimental import pallas as pl
from jax.experimental.pallas import tpu as pltpu
from jax.sharding import PartitionSpec as P


BF = jnp.bfloat16
F32 = jnp.float32
ANY = pl.BlockSpec(memory_space=pl.ANY)
HBM = pl.BlockSpec(memory_space=pltpu.HBM)
VM = pl.BlockSpec(memory_space=pltpu.VMEM)
SM = pl.BlockSpec(memory_space=pltpu.SMEM)
MIB = 1024 * 1024


def swap(x, axis, n, r):
    return lax.ppermute(x, axis, [(i, i ^ r) for i in range(n)])


def tile_of(n, most):
    t = min(n, most)
    while n % t:
        t //= 2
    return t


def tiles(n, most=512):
    return [(i, min(most, n - i)) for i in range(0, n, most)]


def call(kernel, out_shape, in_specs, args, flops=0, moved=0, scratch=(), limit=4, out_specs=None):
    return pl.pallas_call(
        kernel,
        out_shape=out_shape,
        in_specs=in_specs,
        out_specs=jax.tree.map(lambda _: VM, out_shape) if out_specs is None else out_specs,
        scratch_shapes=list(scratch),
        compiler_params=pltpu.CompilerParams(vmem_limit_bytes=limit * MIB),
        cost_estimate=pl.CostEstimate(
            flops=int(flops), bytes_accessed=int(moved), transcendentals=0
        ),
    )(*args)


def shape(dims, dtype=BF):
    return jax.ShapeDtypeStruct(tuple(dims), dtype)


def dot(a, b):
    return jnp.dot(a, b, preferred_element_type=F32)


def whole(ref):
    return ref[...].astype(F32)


def pack_kernel(ne, sc, tokens, ids_in, gates_in, out, ids, gates, sem):
    rows, width = tokens.shape
    copies = [
        pltpu.make_async_copy(src, dst, sem.at[n])
        for n, (src, dst) in enumerate(
            ((ids_in, ids), (gates_in, gates), (tokens, out.at[:, pl.ds(0, width)]))
        )
    ]
    for c in copies:
        c.start()
    for c in copies:
        c.wait()
    g = gates[...]
    share = g / jnp.sum(g, axis=0, keepdims=True)
    lines = lax.broadcasted_iota(jnp.int32, (128, rows), 0)
    w = jnp.zeros(lines.shape, F32)
    for k in range(ids.shape[0]):
        w = w + jnp.where(ids[k : k + 1, :] == lines % ne, share[k : k + 1, :], 0.0)
    high = w.astype(BF).astype(F32)
    middle = (w - high).astype(BF).astype(F32)
    low = w - high - middle
    terms = jnp.where(lines < ne, high, jnp.where(lines < 2 * ne, middle, low))
    terms = jnp.where(lines < 3 * ne, terms, 0.0)
    out[:, width:] = terms.T.astype(BF)


def pack(sc, tokens, ids, gates, ne):
    rows, width = tokens.shape
    return call(
        functools.partial(pack_kernel, ne),
        shape((rows, width + 128)),
        [SM, HBM, HBM, HBM],
        (sc, *map(in_hbm, (tokens, ids.T, gates.T))),
        moved=4 * rows * width,
        scratch=[
            pltpu.VMEM(ids.shape[::-1], jnp.int32),
            pltpu.VMEM(gates.shape[::-1], F32),
            pltpu.SemaphoreType.DMA((3,)),
        ],
    )


def in_hbm(x):
    return pltpu.with_memory_space_constraint(x, pltpu.HBM)


def load_kernel(*refs):
    n = (len(refs) - 2) // 2
    copies = [
        pltpu.make_async_copy(refs[1 + k], refs[1 + n + k], refs[-1].at[k]) for k in range(n)
    ]
    for c in copies:
        c.start()
    for c in copies:
        c.wait()


def load(after, weights):
    return call(
        load_kernel,
        [shape(w.shape) for w in weights],
        [ANY] + [HBM] * len(weights),
        (after, *map(in_hbm, weights)),
        moved=2 * sum(w.size for w in weights),
        scratch=[pltpu.SemaphoreType.DMA((len(weights),))],
        limit=1,
    )


def stack_kernel(*refs):
    out, n = refs[-1], refs[0].shape[0]
    for i, r in enumerate(refs[:-1]):
        out[i * n : (i + 1) * n] = r[...]


def stack(xs):
    n, width = xs[0].shape
    return call(
        stack_kernel, shape((n * len(xs), width)), [VM] * len(xs), xs, moved=4 * len(xs) * n * width
    )


def part_of(hs, nd):
    return hs if hs % (128 * nd) else hs // nd


def units(sc, other, part, hs):
    start = 0 if part == hs else ((1 - sc[0]) if other else sc[0]) * part
    return pl.ds(pl.multiple_of(start, 128), part) if part != hs else pl.ds(0, hs)


def up_kernel(nd, ne, nz, rows, width, sc, tg, tu, sg_in, su_in, td_in, sd_in, *rest):
    count = nd * ne
    own, line = rest[:count], rest[count : 2 * count]
    at_ref, act_ref, f1_ref, f2_ref, xs, td, sd = rest[2 * count : 2 * count + 7]
    sg, su, dsem = rest[2 * count + 7 :]
    bt, bs = tile_of(tg.shape[2], 256), tile_of(sg.shape[1], 256)
    hidden = units(sc, False, sg.shape[1], sg_in.shape[1])
    nt, ns = tg.shape[2] // bt, sg.shape[1] // bs

    def row_of(n):
        return pl.multiple_of((n % ne * nd + (sc[0] ^ (n // ne))) * rows, rows)

    ahead = [
        pltpu.make_async_copy(src, dst, dsem.at[k])
        for k, (src, dst) in enumerate(((sg_in.at[:, hidden], sg), (su_in.at[:, hidden], su), (td_in, td), (sd_in, sd)))
    ]
    for c in ahead:
        c.start()

    for n in range(count):
        for j in range(nz):
            rows_at = pl.ds(row_of(n), rows)
            cols_at = pl.ds(pl.multiple_of((sc[2] ^ j) * width, 128), width)
            xs[rows_at, cols_at] = line[n][(j - 1) * rows : j * rows] if j else own[n][:, :width]

    weights = []
    for b in range(ne):
        pair = []
        for a in range(nd):
            m = own[a * ne + b][:, width:].astype(F32)
            lanes = lax.broadcasted_iota(jnp.int32, m.shape, 1)
            ours = (lanes % ne == sc[1]) & (lanes < 3 * ne)
            pair.append(jnp.sum(jnp.where(ours, m, 0.0), axis=1, keepdims=True))
        for d in range(nd):
            value = pair[0]
            for a in range(1, nd):
                value = jnp.where((sc[0] ^ a) == d, pair[a], value)
            weights.append(value)
    w = jnp.concatenate(weights, axis=0)

    cut = tile_of(nz * width, 1280)
    cuts = [slice(k, k + cut) for k in range(0, nz * width, cut)]

    @pl.loop(0, nt)
    def _(i):
        at = pl.ds(pl.multiple_of(i * bt, bt), bt)
        g = sum(dot(xs[:, k], tg[0, k, at]) for k in cuts)
        u = sum(dot(xs[:, k], tu[0, k, at]) for k in cuts)
        a = g * jax.nn.sigmoid(g) * u
        at_ref[:, at] = jnp.where(w != 0.0, -w * a, 0.0).astype(BF)

    for c in ahead[:2]:
        c.wait()

    @pl.loop(0, ns)
    def _(i):
        at = pl.ds(pl.multiple_of(i * bs, bs), bs)
        g = sum(dot(xs[:, k], sg[k, at]) for k in cuts)
        u = sum(dot(xs[:, k], su[k, at]) for k in cuts)
        s = jax.nn.sigmoid(g)
        f2 = g * s
        act_ref[:, at] = (f2 * u).astype(BF)
        f1_ref[:, at] = u * s * (1.0 + g * (1.0 - s))
        f2_ref[:, at] = f2

    for c in ahead[2:]:
        c.wait()


def up(sc, tg, tu, sg, su, td, sd, own, line, dims):
    nd, ne, nz, rows, width = dims
    total, model = rows * nd * ne, width * nz
    ht, hs = tg.shape[2], part_of(sg.shape[1], nd)
    count = nd * ne
    return call(
        functools.partial(up_kernel, nd, ne, nz, rows, width),
        [
            shape((total, ht)),
            shape((total, hs)),
            shape((total, hs), F32),
            shape((total, hs), F32),
            shape((total, model)),
            shape(td.shape),
            shape(sd.shape),
        ],
        [SM] + [VM] * 2 + [HBM] * 4 + [VM] * (2 * count),
        (sc, tg, tu, *map(in_hbm, (sg, su, td, sd)), *own, *line),
        flops=4 * total * model * (ht + hs),
        moved=2 * total * model,
        scratch=[
            pltpu.VMEM((model, hs), BF),
            pltpu.VMEM((model, hs), BF),
            pltpu.SemaphoreType.DMA((4,)),
        ],
        limit=8 + total // 64,
    )


def rest_kernel(sc, xs, sg_in, su_in, act_ref, f1_ref, f2_ref, sg, su, sem):
    model, hs = sg.shape
    hidden = units(sc, True, hs, sg_in.shape[1])
    cut = tile_of(model, 1280)
    cuts = [slice(k, k + cut) for k in range(0, model, cut)]
    copies = [
        [
            pltpu.make_async_copy(src.at[k, hidden], dst.at[k], sem.at[m, n])
            for m, (src, dst) in enumerate(((sg_in, sg), (su_in, su)))
        ]
        for n, k in enumerate(cuts)
    ]
    for line in copies:
        for c in line:
            c.start()
    g = u = jnp.zeros(act_ref.shape, F32)
    for line, k in zip(copies, cuts):
        for c in line:
            c.wait()
        g = g + dot(xs[:, k], sg[k])
        u = u + dot(xs[:, k], su[k])
    s = jax.nn.sigmoid(g)
    f2 = g * s
    act_ref[...] = (f2 * u).astype(BF)
    f1_ref[...] = u * s * (1.0 + g * (1.0 - s))
    f2_ref[...] = f2


def rest_of_student(sc, xs, sg, su, nd):
    total, model = xs.shape
    hs = part_of(sg.shape[1], nd)
    n = model // tile_of(model, 1280)
    return call(
        rest_kernel,
        [shape((total, hs)), shape((total, hs), F32), shape((total, hs), F32)],
        [SM, VM, HBM, HBM],
        (sc, xs, in_hbm(sg), in_hbm(su)),
        flops=4 * total * model * hs,
        moved=4 * model * hs,
        scratch=[
            pltpu.VMEM((model, hs), BF),
            pltpu.VMEM((model, hs), BF),
            pltpu.SemaphoreType.DMA((2, n)),
        ],
        limit=9,
    )


def down_kernel(kept, student, base, nd, sc, at, act, td, sd, out):
    half = td.shape[2] // nd
    rows = units(sc, False, act.shape[1], sd.shape[0])
    for i, width in tiles(out.shape[1]):
        start = (sc[0] if kept else 1 - sc[0]) * half + base + i
        cols = pl.ds(pl.multiple_of(start, 128), width)
        p = dot(at[...], td[0, :, cols])
        if student:
            p = p + dot(act[...], sd[rows, cols])
        out[:, i : i + width] = p.astype(out.dtype)


def down(sc, at, act, td, sd, base, width, nd, kept):
    total, ht = at.shape
    student = kept or act.shape[1] < sd.shape[0]
    return call(
        functools.partial(down_kernel, kept, student, base, nd),
        shape((total, width), F32 if kept else BF),
        [SM] + [VM] * 4,
        (sc, at, act, td, sd),
        flops=2 * total * width * (ht + act.shape[1] * student),
        moved=2 * total * width,
        limit=4,
    )


def blocks_kernel(own, got, *outs):
    rb = outs[0].shape[0]
    for b, out in enumerate(outs):
        rows = slice(b * rb, (b + 1) * rb)
        out[...] = (own[rows] + got[rows].astype(F32)).astype(BF)


def blocks(own, got, ne):
    total, width = own.shape
    return call(
        blocks_kernel,
        [shape((total // ne, width))] * ne,
        [VM, VM],
        (own, got),
        moved=8 * total * width,
    )


def lines_kernel(ne, sc, own, got, *outs):
    nz = len(outs)
    rb = own.shape[0] // ne
    rp = rb // nz
    for j, out in enumerate(outs):
        for b in range(ne):
            rows = pl.ds(pl.multiple_of(b * rb + (sc[2] ^ j) * rp, rp), rp)
            out[b * rp : (b + 1) * rp] = (own[rows, :] + got[rows, :].astype(F32)).astype(BF)


def line_blocks(sc, own, got, ne, nz):
    total, width = own.shape
    return call(
        functools.partial(lines_kernel, ne),
        [shape((total // nz, width))] * nz,
        [SM, VM, VM],
        (sc, own, got),
        moved=8 * total * width,
    )


def sum_kernel(pick, count, sc, *refs):
    parts, outs = refs[:count], refs[count:]
    rp = outs[0].shape[0]
    for j, out in enumerate(outs):
        first = (sc[2] ^ j) * rp if pick else j * rp
        rows = pl.ds(pl.multiple_of(first, rp), rp)
        out[...] = sum(p[rows, :].astype(F32) for p in parts).astype(BF)


def sum_parts(sc, parts, n, pick):
    rb, width = parts[0].shape
    return call(
        functools.partial(sum_kernel, pick, len(parts)),
        [shape((rb // n, width))] * n,
        [SM] + [VM] * len(parts),
        (sc, *parts),
        moved=4 * len(parts) * rb * width,
    )


def final_kernel(counts, scale, *refs):
    out, at, col = refs[-1], 0, 0
    for n in counts:
        parts = refs[at : at + n]
        width = parts[0].shape[1]
        out[:, col : col + width] = (sum(whole(p) for p in parts) * scale).astype(BF)
        at, col = at + n, col + width


def final(groups, scale):
    rp = groups[0][0].shape[0]
    width = sum(g[0].shape[1] for g in groups)
    flat = [p for g in groups for p in g]
    return call(
        functools.partial(final_kernel, [len(g) for g in groups], scale),
        shape((rp, width)),
        [VM] * len(flat),
        flat,
        moved=8 * rp * width,
    )


def back_kernel(nd, ne, nz, groups, model_tokens, grad_scale, sc, sd, x_in, *rest):
    count = nd * ne
    forward, rest = rest[: 3 * groups], rest[3 * groups :]
    own, line = rest[:count], rest[count : 2 * count]
    gg, gu, gd, loss = rest[2 * count : 2 * count + 4]
    xs, d_ref, act_t, sq, dpre, dbuf, xbuf, xsem, dsem, gsem = rest[2 * count + 4 :]
    rp, half = own[0].shape
    total, hs = d_ref.shape[0], sd.shape[0]
    model = half * nd
    rb = total // ne
    part = hs // groups
    second = sc[0] == 1

    def kind(k):
        if groups == 1:
            return [forward[k][...]]
        mine, other = forward[k][...], forward[3 + k][...]
        return [jnp.where(second, other, mine), jnp.where(second, mine, other)]

    fetch = pltpu.make_async_copy(x_in, xs, xsem)
    fetch.start()
    for h, act in enumerate(kind(0)):
        act_t[h * part : (h + 1) * part] = act.T
    for n in range(count):
        cols = pl.ds(pl.multiple_of((sc[0] ^ (n // ne)) * half, 128), half)
        for j in range(nz):
            at = pl.ds(pl.multiple_of(n % ne * rb + (sc[2] ^ j) * rp, rp), rp)
            d_ref[at, cols] = line[n][(j - 1) * rp : j * rp] if j else own[n][...]
    bn = dbuf.shape[2]
    n = model // bn
    dact = jnp.zeros((total, hs), F32)
    out = []
    s = jnp.zeros((total, 128), F32)
    for i in range(n):
        here = slice(i * bn, (i + 1) * bn)
        dbuf[i] = dot(act_t[...], d_ref[:, here]).astype(BF)
        out.append(pltpu.make_async_copy(dbuf.at[i], gd.at[:, here], dsem.at[i]))
        out[-1].start()
        dact = dact + lax.dot_general(
            d_ref[:, here], sd[:, here], (((1,), (1,)), ((), ())), preferred_element_type=F32
        )
        f = d_ref[:, here].astype(F32)
        for k in range(bn // 128):
            lane = f[:, k * 128 : (k + 1) * 128]
            s = s + lane * lane
    for k in range(2):
        for h, f in enumerate(kind(1 + k)):
            d = dact[:, h * part : (h + 1) * part]
            dpre[:, k * hs + h * part : k * hs + (h + 1) * part] = (d * f).astype(BF)
    fetch.wait()
    for i in range(n):
        here = slice(i * bn, (i + 1) * bn)
        both = lax.dot_general(
            xs[:, here], dpre[...], (((0,), (0,)), ((), ())), preferred_element_type=F32
        ).astype(BF)
        for k, g in enumerate((gg, gu)):
            at = 2 * i + k
            xbuf[at] = both[:, k * hs : (k + 1) * hs]
            out.append(pltpu.make_async_copy(xbuf.at[at], g.at[here, :], gsem.at[at]))
            out[-1].start()
    sq[...] = s
    tot = jnp.zeros((rb, 128), F32)
    for e in range(ne):
        tot = tot + sq[pl.ds(pl.multiple_of((sc[1] ^ e) * rb, rb), rb), :]
    value = jnp.sum(jnp.sum(tot, axis=0, keepdims=True), axis=1, keepdims=True)
    loss[...] = value * (1.0 / (grad_scale * grad_scale)) / model_tokens
    for c in out:
        c.wait()


def back(sc, forward, sd, xs, own, line, dims, model_tokens, grad_scale):
    nd, ne, nz = dims
    total, hs = xs.shape[0], sd.shape[0]
    model = sd.shape[1]
    bn = tile_of(model, 1280)
    n = model // bn
    return call(
        functools.partial(back_kernel, nd, ne, nz, len(forward) // 3, model_tokens, grad_scale),
        [shape((model, hs)), shape((model, hs)), shape((hs, model)), shape((1, 1), F32)],
        [SM, VM, ANY] + [VM] * (len(forward) + 2 * nd * ne),
        (sc, sd, xs, *forward, *own, *line),
        flops=8 * total * model * hs,
        moved=6 * model * hs,
        scratch=[
            pltpu.VMEM((total, model), BF),
            pltpu.VMEM((total, model), BF),
            pltpu.VMEM((hs, total), BF),
            pltpu.VMEM((total, 128), F32),
            pltpu.VMEM((total, 2 * hs), BF),
            pltpu.VMEM((n, hs, bn), BF),
            pltpu.VMEM((2 * n, bn, hs), BF),
            pltpu.SemaphoreType.DMA,
            pltpu.SemaphoreType.DMA((n,)),
            pltpu.SemaphoreType.DMA((2 * n,)),
        ],
        out_specs=[HBM, HBM, HBM, VM],
        limit=25,
    )


def body(tokens, expert_ids, gate_weights, t_gate, t_up, t_down, s_gate, s_up, s_down):
    nd, ne, nz = lax.axis_size("dp"), lax.axis_size("expert"), lax.axis_size("tensor")
    rows, width = tokens.shape
    model = width * nz
    total = rows * ne * nd
    sc = jnp.stack(
        [lax.axis_index("dp"), lax.axis_index("expert"), lax.axis_index("tensor")]
    ).astype(jnp.int32)

    def spread(x, packed):
        line = [swap(x, "tensor", nz, j) for j in range(1, nz)]
        own = [packed] + [swap(packed, "expert", ne, b) for b in range(1, ne)]
        line = stack(line)
        lines = [line] + [swap(line, "expert", ne, b) for b in range(1, ne)]
        own += [swap(z, "dp", nd, 1) for z in own]
        lines += [swap(z, "dp", nd, 1) for z in lines]
        return own, lines

    own, lines = spread(tokens, pack(sc, tokens, expert_ids, gate_weights, ne))
    loaded = []
    for w in (t_gate, t_up):
        loaded += load(lines[0], (w,))
    at, *forward, xs, td, sd = up(
        sc, *loaded, s_gate, s_up, t_down, s_down, own, lines, (nd, ne, nz, rows, width)
    )
    act = forward[0]
    if act.shape[1] < sd.shape[0]:
        forward += rest_of_student(sc, xs, s_gate, s_up, nd)

    half = model // nd
    cut = half - max(128, half * 3 // 10 // 128 * 128)
    parts = ((0, cut), (cut, half - cut))
    sent = [down(sc, at, act, td, sd, *p, nd, False) for p in parts]
    got = [swap(s, "dp", nd, 1) for s in sent]
    kept = [down(sc, at, act, td, sd, *p, nd, True) for p in parts]

    def over(xs, axis, n):
        return [xs[0]] + [swap(xs[k], axis, n, k) for k in range(1, n)]

    wide = over(blocks(kept[0], got[0], ne), "expert", ne)
    slim = over(line_blocks(sc, kept[1], got[1], ne, nz), "tensor", nz)
    slim = sum_parts(sc, slim, ne, False)
    slim = over(slim, "expert", ne)
    wide = sum_parts(sc, wide, nz, True)
    wide = over(wide, "tensor", nz)
    grad_scale = 1.0 / math.sqrt(total)
    d_out = final((wide, slim), grad_scale)

    own, lines = spread(d_out, d_out)
    gg, gu, gd, loss = back(
        sc, forward, sd, xs, own, lines, (nd, ne, nz), total * model, grad_scale
    )
    return gg, gu, gd, loss[0, 0]


def solution(mesh):
    return jax.shard_map(
        body,
        mesh=mesh,
        in_specs=(
            P(("dp", "expert"), "tensor"),
            P(("dp", "expert"), None),
            P(("dp", "expert"), None),
            P("expert", None, ("dp", "tensor")),
            P("expert", None, ("dp", "tensor")),
            P("expert", ("dp", "tensor"), None),
            P(None, ("expert", "tensor")),
            P(None, ("expert", "tensor")),
            P(("expert", "tensor"), None),
        ),
        out_specs=(
            P(None, ("expert", "tensor")),
            P(None, ("expert", "tensor")),
            P(("expert", "tensor"), None),
            P(),
        ),
        check_vma=False,
    )
```
